512 devices in a mesh: samp: 64 (over z, y_hi, core), var: 8 (over x, y_lo).
Axes of the slice: x: 4, y: 8 (y_hi: 4, y_lo: 2; y = y_hi * 2 + y_lo), z: 8, core: 2. Of those that a mesh axis runs over, the one named last changes fastest.
Arguments:
- dosages: bfloat16 [32768, 14336], P('samp', 'var'), may hold values from 0 to 2
- weights: bfloat16 [14336, 512], P('var'), may hold values from -0.046875 to 0.046875
- prior: float32 [32768, 512], P('samp', 'var'), may hold values from -16 to 16
- cohort: int32 [32768, 1], P('samp'), may hold values from 0 to 15
- expression: bfloat16 [32768, 10240], P('samp', 'var'), may hold values from -6 to 6
Outputs:
- correlation: float32 [512, 10240], P('samp', 'var')
The draws below stay inside these ranges and needn't reach their ends.
Inputs may be any that keep to these rules, and one draw needn't show every extreme that they name: Every cohort has at least one sample.
All inputs are finite; a program needn't handle non-finite values.
Results may differ from the reference program's by a relative error of at most 0.0042.
Values may be sent and summed in bfloat16 or wider, within the bound.
A program may use at most 64 MiB of HBM per device.

```python
import jax
import jax.numpy as jnp
from jax import lax

K = 512
GENES = 10240
COHORTS = 16
SAMPLES = 32768
VARIANTS = 14336


def with_spikes(result, rng, source, target, blocks, factor):
    owner, partner = [(jnp.arange(result.shape[dim]) // (result.shape[dim] // blocks)).reshape([-1 if axis == dim else 1 for axis in range(result.ndim)]) for dim in (source, target)]
    chosen = jax.random.permutation(rng, blocks)[partner]
    strong = (owner == chosen) | (owner == (partner + blocks // 2) % blocks)
    return jnp.where(strong, factor * result, result)


def steps_of(rng, extent, cuts, least, high):
    def one(dim, shards_of):
        steps = jax.random.uniform(jax.random.fold_in(jax.random.fold_in(rng, 6), dim), (shards_of,), jnp.float32, least / len(cuts), high / len(cuts))
        return jnp.repeat(jnp.exp(steps), extent[dim] // shards_of).reshape((-1,) + (1,) * (len(extent) - dim - 1))

    gain = one(*cuts[0])
    for cut in cuts[1:]:
        gain = gain * one(*cut)
    return gain


def different_ones(key, rows, number_of, top, lift):
    order = jax.random.permutation(jax.random.fold_in(key, 1), number_of)
    favour = order
    for power in range(3):
        favour = favour * favour // number_of
    favour = favour * lift // number_of
    chance = jax.random.randint(jax.random.fold_in(key, 2), (rows, number_of), 0, 4096) + favour
    fixed_rows = jax.random.permutation(jax.random.fold_in(key, 3), rows)[jnp.arange(number_of) % rows]
    chance = jnp.where(jnp.arange(rows)[:, None] == fixed_rows[None, :], 1 << 14, chance)
    merit = chance * number_of + jnp.arange(number_of)
    return lax.top_k(merit.astype(jnp.int32), top)[1].astype(jnp.int32)


def scatter_about(key, shape, scale, bound, split=(), kind=jnp.bfloat16):
    gain = steps_of(key, shape, split, -0.22, 0.18) if split else 1.0
    drawn = jax.random.normal(key, shape, jnp.float32) * scale * gain
    return jnp.minimum(jnp.maximum(drawn, -bound), bound).astype(kind)


def noise_with(own_key, dims, scale, bound, cuts, heavy, kind=jnp.bfloat16):
    result = scale * jax.random.normal(own_key, dims, jnp.float32)
    if cuts:
        result = result * steps_of(own_key, dims, cuts, -0.22, 0.18)
    return jnp.clip(with_spikes(result, jax.random.fold_in(own_key, 3), *heavy), -bound, bound).astype(kind)


def setup_inputs(seed: int = 0) -> dict:
    splits = jax.random.split(jax.random.key(seed), 6)
    return {
        "dosages": jnp.clip(2.0 * jax.random.uniform(splits[0], (SAMPLES, VARIANTS), jnp.float32) ** steps_of(splits[0], (SAMPLES, VARIANTS), ((0, 64), (1, 8)), -0.2, 0.2), 0.0, 2.0).astype(jnp.bfloat16),
        "weights": scatter_about(splits[1], (VARIANTS, K), VARIANTS ** -0.5, 0.046875, ((0, 8),)),
        "prior": noise_with(splits[2], (SAMPLES, K), 1.0, 16.0, ((0, 64), (1, 8)), (0, 1, 64, 4.0), jnp.float32),
        "cohort": different_ones(splits[3], SAMPLES, COHORTS, 1, 512),
        "expression": scatter_about(splits[4], (SAMPLES, GENES), 1.0, 6.0, ((0, 64), (1, 8))),
    }


def reference(dosages, weights, prior, cohort, expression):
    scores = prior + jnp.dot(dosages, weights, preferred_element_type=jnp.float32)
    onehot = (cohort == jnp.arange(COHORTS, dtype=jnp.int32)[None, :]).astype(jnp.float32)
    counts = lax.optimization_barrier(jnp.sum(onehot, axis=0))
    sums = jnp.dot(onehot.T, scores, precision=lax.Precision.HIGHEST)
    means = sums / counts[:, None]
    centered = scores - means[cohort[:, 0]]
    spread = lax.rsqrt(lax.optimization_barrier(jnp.sum(centered * centered, axis=0)) / SAMPLES + 1e-06)
    standard = (centered * spread[None, :]).astype(jnp.bfloat16)
    cross = jnp.dot(standard.T, expression, preferred_element_type=jnp.float32)
    return cross / SAMPLES
```

```python
import functools

import jax
import jax.numpy as jnp
from jax import lax
from jax.experimental import pallas as pl
from jax.experimental.pallas import tpu as pltpu
from jax.sharding import PartitionSpec as P

COHORTS = 16
MESH = pl.DeviceIdType.MESH
F32 = jnp.float32
BF16 = jnp.bfloat16
NX, NL, NZ, NY, NC = 4, 2, 8, 4, 2
VAR = [(dx, dl) for dx in (2, 1, 3, 0) for dl in (1, 0) if dx or dl]
YC = [(dy, dc) for dy in (2, 1, 3, 0) for dc in (1, 0) if dy or dc]
ZD = [4, 3, 5, 2, 6, 1, 7]


def split2(a):
    hi = a.astype(BF16)
    return hi, (a - hi.astype(F32)).astype(BF16)


def split3(a):
    hi = a.astype(BF16)
    rest = a - hi.astype(F32)
    mid = rest.astype(BF16)
    return hi, mid, (rest - mid.astype(F32)).astype(BF16)


def dot(a, b):
    return jnp.dot(a, b, preferred_element_type=F32)


def dot_t(a, b):
    return lax.dot_general(a, b, (((0,), (0,)), ((), ())), preferred_element_type=F32)


def dot_nt(a, b):
    return lax.dot_general(a, b, (((1,), (1,)), ((), ())), preferred_element_type=F32)


def kernel(
    total, d_hbm, w_hbm, p_hbm, co_hbm, e_hbm, o_ref,
    d, w, p, co, e_all, lt, rt, snd, own, rs_buf, x_all, st_src, st_buf, t_src, yc_buf, t2_src, z_buf,
    d_src, dm, cross, cb, zx_buf, ysrc, yx_buf, q_src, q_yc, q2_src, q_z,
    ld, e_sem, st_s, st_r, yc_s, yc_r, z_s, z_r, dm_s, dm_r, rs_s, rs_r, ag_s, ag_r, sb_s, sb_r,
    zx_s, zx_r, yx_s, yx_r, qy_s, qy_r, qz_s, qz_r,
):
    samp, var = lax.axis_index("samp"), lax.axis_index("var")
    z, y, c = samp // 8, (samp // 2) % 4, samp % 2
    x, l = var // 2, var % 2
    nv = NX * NL
    rows = d.shape[0]
    blk = rows // nv
    k = w.shape[1]
    half = e_all.shape[1]
    zrows = k // NZ

    def var_of(dx, dl):
        return ((x + dx) % NX) * NL + (l + dl) % NL

    def samp_of(dz, dy, dc):
        return ((z + dz) % NZ) * 8 + ((y + dy) % NY) * 2 + (c + dc) % NC

    sib = (samp_of(0, 0, 1), var)

    def remote(src, dst, ss, rs, dev):
        cp = pltpu.make_async_remote_copy(
            src_ref=src, dst_ref=dst, send_sem=ss, recv_sem=rs, device_id=dev, device_id_type=MESH
        )
        cp.start()
        return cp

    def local(src, dst, sem):
        cp = pltpu.make_async_copy(src, dst, sem)
        cp.start()
        return cp

    barrier = pltpu.get_barrier_semaphore()
    peers = (
        [(samp, var_of(*q)) for q in VAR]
        + [(samp_of(0, 0, 1), var_of(*q)) for q in VAR]
        + [(samp_of(0, *q), var) for q in YC]
        + [(samp_of(q, 0, 0), var) for q in ZD]
    )
    for dev in peers:
        pl.semaphore_signal(barrier, inc=1, device_id=dev, device_id_type=MESH)

    cp_co = local(co_hbm, co.at[0], ld.at[0])
    cp_d = local(d_hbm, d, ld.at[1])
    cp_w = local(w_hbm, w, ld.at[2])
    cp_p = local(p_hbm, p, ld.at[3])
    mine = pl.multiple_of(c * half, 128)
    other = pl.multiple_of((1 - c) * half, 128)
    cp_e = local(e_hbm.at[:, pl.ds(mine, half)], e_all.at[pl.ds(0, rows)], ld.at[4])

    cp_co.wait()
    cohorts = lax.broadcasted_iota(jnp.int32, (COHORTS, rows), 0)
    hot = (co[0] == cohorts).astype(F32)
    oh = hot.astype(BF16)
    count = jnp.sum(hot, axis=1, keepdims=True)
    cp_p.wait()
    p3 = split3(p[...])
    width = p.shape[0]
    for i in range(3):
        lt[i * width : (i + 1) * width] = p3[i]
        lt[3 * width + i * COHORTS : 3 * width + (i + 1) * COHORTS] = oh
    lt[3 * width + 3 * COHORTS :] = jnp.zeros((COHORTS, rows), BF16)
    sel = lax.broadcasted_iota(jnp.int32, (width, k), 1) - var * width == lax.broadcasted_iota(jnp.int32, (width, k), 0)
    sel = sel.astype(F32).astype(BF16)
    ps = [dot_nt(oh, p3[i]) for i in range(3)]
    ps = ps[0] + ps[1] + ps[2]
    ps = sum(dot(part, sel) for part in split3(ps))
    cp_d.wait()
    a3 = split3(dot(oh, d[...]))
    cp_w.wait()
    sums = ps + sum(dot(part, w[...]) for part in a3)
    m3 = split3(-sums / jnp.maximum(count, 1.0))
    for i in range(3):
        rt[i * width : (i + 1) * width] = sel
        rt[3 * width + i * COHORTS : 3 * width + (i + 1) * COHORTS] = m3[i]
    rt[3 * width + 3 * COHORTS :] = jnp.zeros((COHORTS, k), BF16)
    lane = lax.broadcasted_iota(jnp.int32, (COHORTS, 128), 1)
    low = lane < width
    for j in range(k // 128):
        pair = sums[:, j * 128 : (j + 1) * 128]
        st_src[2 * j] = jnp.where(low, pair, count)
        st_src[2 * j + 1] = jnp.where(low, pltpu.roll(pair, 64, 1), count)

    pl.semaphore_wait(barrier, len(peers))
    cp_e2 = remote(e_hbm.at[:, pl.ds(other, half)], e_all.at[pl.ds(rows, rows)], e_sem.at[0], e_sem.at[1], sib)
    cp_co2 = remote(co_hbm, co.at[1], e_sem.at[2], e_sem.at[3], sib)
    st = [
        remote(st_src.at[var_of(*q)], st_buf.at[i], st_s.at[i], st_r.at[i], (samp, var_of(*q)))
        for i, q in enumerate(VAR)
    ]

    rs = []
    for step, dx in enumerate((2, 1, 3, 0)):
        xo = (x + dx) % NX
        r0 = pl.multiple_of(xo * (2 * blk), 2 * blk)
        f = dot(d[pl.ds(r0, 2 * blk)], w[...]) + dot_t(lt[:, pl.ds(r0, 2 * blk)], rt[...])
        snd[pl.ds(r0, 2 * blk)] = f.astype(BF16)
        if dx == 0:
            own[...] = f
        for dl in (1, 0):
            if dx or dl:
                i = VAR.index((dx, dl))
                to = var_of(dx, dl)
                rs.append(
                    remote(
                        snd.at[pl.ds(pl.multiple_of(to * blk, blk), blk)], rs_buf.at[i], rs_s.at[i], rs_r.at[i],
                        (samp, to),
                    )
                )

    for cp in st:
        cp.wait_recv()
    t = st_src[var]
    for i in range(len(VAR)):
        t = t + st_buf[i]
    t = jnp.where(low, t, count)
    t_src[...] = t
    ycs = [
        remote(t_src, yc_buf.at[i], yc_s.at[i], yc_r.at[i], (samp_of(0, *q), var)) for i, q in enumerate(YC)
    ]
    cp_e.wait()
    e_own = dot(oh, e_all[pl.ds(0, rows)])
    cp_e2.wait_recv()
    cp_co2.wait_recv()
    oh2 = (co[1] == cohorts).astype(F32).astype(BF16)
    e_sib = dot(oh2, e_all[pl.ds(rows, rows)])

    for cp in rs:
        cp.wait_recv()
    at = pl.multiple_of(l * blk, blk)
    s = own[pl.ds(at, blk)]
    for i in range(len(VAR)):
        s = s + rs_buf[i].astype(F32)
    row = pl.multiple_of(var * blk, blk)
    x_all[pl.ds(row, blk)] = s.astype(BF16)
    ag = [
        remote(x_all.at[pl.ds(row, blk)], x_all.at[pl.ds(row, blk)], ag_s.at[i], ag_r.at[i], (samp, var_of(*q)))
        for i, q in enumerate(VAR)
    ]
    sb = [
        remote(x_all.at[pl.ds(row, blk)], x_all.at[pl.ds(pl.multiple_of(rows + row, blk), blk)], sb_s.at[7], sb_r.at[7], sib)
    ]

    for cp in ycs:
        cp.wait_recv()
    t2 = t
    for i in range(len(YC)):
        t2 = t2 + yc_buf[i]
    t2_src[...] = t2
    zs = [
        remote(t2_src, z_buf.at[i], z_s.at[i], z_r.at[i], (samp_of(q, 0, 0), var)) for i, q in enumerate(ZD)
    ]
    for i in range(len(VAR) - 1, -1, -1):
        dx, dl = VAR[i]
        ag[i].wait_recv()
        got = pl.multiple_of(var_of(-dx, -dl) * blk, blk)
        sb.append(
            remote(
                x_all.at[pl.ds(got, blk)], x_all.at[pl.ds(pl.multiple_of(rows + got, blk), blk)], sb_s.at[i], sb_r.at[i], sib
            )
        )
    for cp in zs:
        cp.wait_recv()
    t3 = t2
    for i in range(len(ZD)):
        t3 = t3 + z_buf[i]
    mean = t3 / pltpu.roll(t3, 64, 1)
    d_src[...] = jnp.where(low, t / jnp.maximum(count, 1.0) - mean, 0.0)
    dm[0, var] = d_src[...]
    dms = []
    for i, q in enumerate(VAR):
        for dc in range(NC):
            n = 2 * i + dc
            dms.append(
                remote(d_src, dm.at[dc, var], dm_s.at[n], dm_r.at[n], (samp_of(0, 0, dc), var_of(*q)))
            )
    dms.append(remote(d_src, dm.at[1, var], dm_s.at[14], dm_r.at[14], sib))

    for cp in sb:
        cp.wait_recv()
    cross[...] = dot_t(x_all[...], e_all[...])
    for cp in dms:
        cp.wait_recv()

    def spread_out(i):
        return jnp.concatenate(
            [jnp.where(low, dm[i, 2 * j], pltpu.roll(dm[i, 2 * j + 1], 64, 1)) for j in range(nv // 2)], axis=1
        )

    d_own = spread_out(0)
    d2 = [split2(d_own), split2(spread_out(1))]
    e2 = [split2(e_own), split2(e_sib)]
    left = jnp.concatenate([d2[i][a] for i in range(2) for a in range(2) for b in range(2)], axis=0)
    right = jnp.concatenate([e2[i][b] for i in range(2) for a in range(2) for b in range(2)], axis=0)
    full = cross[...] + dot_t(left, right)
    cross[...] = full
    cb[...] = full.astype(BF16)
    zx = []
    for i, q in enumerate(ZD):
        to = pl.multiple_of(((z + q) % NZ) * zrows, zrows)
        zx.append(remote(cb.at[pl.ds(to, zrows)], zx_buf.at[i], zx_s.at[i], zx_r.at[i], (samp_of(q, 0, 0), var)))

    xo = x_all[pl.ds(0, rows)]
    xf = xo.astype(F32)
    resid = dot(oh, xo)
    q = jnp.sum(xf * xf, axis=0, keepdims=True)
    q = q + jnp.sum(d_own * (2.0 * resid + count * d_own), axis=0, keepdims=True)
    q_src[...] = jnp.concatenate([q[:, j * 128 : (j + 1) * 128] for j in range(k // 128)] * 2, axis=0)
    qy = [
        remote(q_src, q_yc.at[i], qy_s.at[i], qy_r.at[i], (samp_of(0, *a), var)) for i, a in enumerate(YC)
    ]
    for cp in qy:
        cp.wait_recv()
    q2 = q_src[...]
    for i in range(len(YC)):
        q2 = q2 + q_yc[i]
    q2_src[...] = q2
    qz = [
        remote(q2_src, q_z.at[i], qz_s.at[i], qz_r.at[i], (samp_of(a, 0, 0), var)) for i, a in enumerate(ZD)
    ]

    for cp in zx:
        cp.wait_recv()
    acc = cross[pl.ds(pl.multiple_of(z * zrows, zrows), zrows)]
    for i in range(len(ZD)):
        acc = acc + zx_buf[i].astype(F32)
    for j in range(NY * NC):
        ysrc[j] = acc[j * 8 : (j + 1) * 8]
    yx = []
    for i, (dy, dc) in enumerate(YC):
        to = ((y + dy) % NY) * 2 + (c + dc) % NC
        yx.append(remote(ysrc.at[to], yx_buf.at[i], yx_s.at[i], yx_r.at[i], (samp_of(0, dy, dc), var)))
    for cp in qz:
        cp.wait_recv()
    q3 = q2
    for i in range(len(ZD)):
        q3 = q3 + q_z[i]
    spread = lax.rsqrt(q3[:4] / total + 1e-6) / total
    spread = jnp.concatenate([spread[j : j + 1] for j in range(4)], axis=1)
    at_row = lax.broadcasted_iota(jnp.int32, (8, k), 1) - samp * 8 == lax.broadcasted_iota(jnp.int32, (8, k), 0)
    scale = jnp.sum(jnp.where(at_row, spread, 0.0), axis=1, keepdims=True)

    for cp in yx:
        cp.wait_recv()
    same = ysrc[y * 2 + c]
    cross_half = jnp.zeros_like(same)
    for i, (dy, dc) in enumerate(YC):
        if dc:
            cross_half = cross_half + yx_buf[i]
        else:
            same = same + yx_buf[i]
    o_ref[:, pl.ds(mine, half)] = same * scale
    o_ref[:, pl.ds(other, half)] = cross_half * scale

    for cp in [cp_e2, cp_co2] + st + rs + ycs + ag + sb + zs + dms + zx + qy + qz + yx:
        cp.wait_send()


def shards(total, dosages, weights, prior, cohort, expression):
    rows, depth = dosages.shape
    k = weights.shape[1]
    genes = expression.shape[1]
    half = genes // 2
    width = prior.shape[1]
    blk = rows // 8
    out_rows = k // 64
    vm, sem = pltpu.VMEM, pltpu.SemaphoreType.DMA
    scratch = [
        vm((rows, depth), BF16), vm((depth, k), BF16), vm((width, rows), F32), vm((2, 1, rows), jnp.int32),
        vm((2 * rows, half), BF16), vm((3 * width + 4 * COHORTS, rows), BF16), vm((3 * width + 4 * COHORTS, k), BF16),
        vm((rows, k), BF16), vm((2 * blk, k), F32), vm((7, blk, k), BF16), vm((2 * rows, k), BF16),
        vm((8, COHORTS, 128), F32), vm((7, COHORTS, 128), F32), vm((COHORTS, 128), F32), vm((7, COHORTS, 128), F32),
        vm((COHORTS, 128), F32), vm((7, COHORTS, 128), F32),
        vm((COHORTS, 128), F32), vm((2, 8, COHORTS, 128), F32), vm((k, half), F32), vm((k, half), BF16),
        vm((7, k // 8, half), BF16), vm((8, out_rows, half), F32), vm((7, out_rows, half), F32),
        vm((8, 128), F32), vm((7, 8, 128), F32), vm((8, 128), F32), vm((7, 8, 128), F32),
        sem((5,)), sem((4,)), sem((7,)), sem((7,)), sem((7,)), sem((7,)), sem((7,)), sem((7,)),
        sem((15,)), sem((15,)), sem((7,)), sem((7,)), sem((7,)), sem((7,)), sem((8,)), sem((8,)),
        sem((7,)), sem((7,)), sem((7,)), sem((7,)), sem((7,)), sem((7,)), sem((7,)), sem((7,)),
    ]
    return pl.pallas_call(
        functools.partial(kernel, float(total)),
        out_shape=jax.ShapeDtypeStruct((out_rows, genes), F32),
        in_specs=[pl.BlockSpec(memory_space=pl.ANY)] * 5,
        out_specs=pl.BlockSpec(memory_space=pltpu.VMEM),
        scratch_shapes=scratch,
        compiler_params=pltpu.CompilerParams(
            collective_id=0, has_side_effects=True, vmem_limit_bytes=48 << 20
        ),
    )(dosages, weights, prior.T, cohort.reshape(1, rows), expression)


def solution(mesh):
    placed = (P("samp", "var"), P("var", None), P("samp", "var"), P("samp", None), P("samp", "var"))

    def run(dosages, weights, prior, cohort, expression):
        body = functools.partial(shards, dosages.shape[0])
        return jax.shard_map(body, mesh=mesh, in_specs=placed, out_specs=P("samp", "var"), check_vma=False)(
            dosages, weights, prior, cohort, expression
        )

    return run
```

```python
import functools

import jax
import jax.numpy as jnp
from jax import lax
from jax.experimental import pallas as pl
from jax.experimental.pallas import tpu as pltpu
from jax.sharding import PartitionSpec as P

COHORTS = 16
MESH = pl.DeviceIdType.MESH
F32 = jnp.float32
BF16 = jnp.bfloat16
NX, NL, NZ, NY, NC = 4, 2, 8, 4, 2
VAR = [(dx, dl) for dx in (2, 1, 3, 0) for dl in (1, 0) if dx or dl]
YC = [(dy, dc) for dy in (2, 1, 3, 0) for dc in (1, 0) if dy or dc]
ZD = [4, 3, 5, 2, 6, 1, 7]
DY = (2, 1, 3, 0)


def hops_of(chunk, way):
    return 4 if (chunk + way) % 2 == 0 else 3


def split2(a):
    hi = a.astype(BF16)
    return hi, (a - hi.astype(F32)).astype(BF16)


def split3(a):
    hi = a.astype(BF16)
    rest = a - hi.astype(F32)
    mid = rest.astype(BF16)
    return hi, mid, (rest - mid.astype(F32)).astype(BF16)


def dot(a, b):
    return jnp.dot(a, b, preferred_element_type=F32)


def dot_t(a, b):
    return lax.dot_general(a, b, (((0,), (0,)), ((), ())), preferred_element_type=F32)


def dot_nt(a, b):
    return lax.dot_general(a, b, (((1,), (1,)), ((), ())), preferred_element_type=F32)


def kernel(
    total, d_hbm, w_hbm, p_hbm, co_hbm, e_hbm, o_ref,
    d, w, p, co, e_all, lt, rt, snd, own, rs_buf, x_all, st_src, st_buf, t_src, yc_buf, t2_src, z_buf,
    d_src, dm, cross, cb, zx_buf, zx_src, ysrc, yx_buf, q_src, q_yc, q2_src, q_z,
    ld, e_sem, st_s, st_r, yc_s, yc_r, z_s, z_r, dm_s, dm_r, rs_s, rs_r, ag_s, ag_r, sb_s, sb_r,
    zx_s, zx_r, yx_s, yx_r, qy_s, qy_r, qz_s, qz_r,
):
    samp, var = lax.axis_index("samp"), lax.axis_index("var")
    z, y, c = samp // 8, (samp // 2) % 4, samp % 2
    x, l = var // 2, var % 2
    nv = NX * NL
    rows = d.shape[0]
    blk = rows // nv
    k = w.shape[1]
    half = e_all.shape[1]
    zrows = k // NZ

    def var_of(dx, dl):
        return ((x + dx) % NX) * NL + (l + dl) % NL

    def samp_of(dz, dy, dc):
        return ((z + dz) % NZ) * 8 + ((y + dy) % NY) * 2 + (c + dc) % NC

    sib = (samp_of(0, 0, 1), var)

    def remote(src, dst, ss, rs, dev):
        cp = pltpu.make_async_remote_copy(
            src_ref=src, dst_ref=dst, send_sem=ss, recv_sem=rs, device_id=dev, device_id_type=MESH
        )
        cp.start()
        return cp

    def local(src, dst, sem):
        cp = pltpu.make_async_copy(src, dst, sem)
        cp.start()
        return cp

    barrier = pltpu.get_barrier_semaphore()
    peers = (
        [(samp, var_of(*q)) for q in VAR]
        + [(samp_of(0, 0, 1), var_of(*q)) for q in VAR]
        + [(samp_of(0, *q), var) for q in YC]
        + [(samp_of(q, 0, 0), var) for q in ZD]
    )
    for dev in peers:
        pl.semaphore_signal(barrier, inc=1, device_id=dev, device_id_type=MESH)

    cp_co = local(co_hbm, co.at[0], ld.at[0])
    cp_p = local(p_hbm, p, ld.at[3])
    cp_d = local(d_hbm, d, ld.at[1])
    cp_w = local(w_hbm, w, ld.at[2])
    mine = pl.multiple_of(c * half, 128)
    other = pl.multiple_of((1 - c) * half, 128)

    cp_co.wait()
    cohorts = lax.broadcasted_iota(jnp.int32, (COHORTS, rows), 0)
    hot = (co[0] == cohorts).astype(F32)
    oh = hot.astype(BF16)
    count = jnp.sum(hot, axis=1, keepdims=True)
    cp_p.wait()
    p3 = split3(p[...])
    width = p.shape[0]
    for i in range(3):
        lt[i * width : (i + 1) * width] = p3[i]
        lt[3 * width + i * COHORTS : 3 * width + (i + 1) * COHORTS] = oh
    lt[3 * width + 3 * COHORTS :] = jnp.zeros((COHORTS, rows), BF16)
    sel = lax.broadcasted_iota(jnp.int32, (width, k), 1) - var * width == lax.broadcasted_iota(jnp.int32, (width, k), 0)
    sel = sel.astype(F32).astype(BF16)
    ps = [dot_nt(oh, p3[i]) for i in range(3)]
    ps = ps[0] + ps[1] + ps[2]
    ps = sum(dot(part, sel) for part in split3(ps))
    cp_d.wait()
    a3 = split3(dot(oh, d[...]))
    cp_w.wait()
    sums = ps + sum(dot(part, w[...]) for part in a3)
    m3 = split3(-sums / jnp.maximum(count, 1.0))
    for i in range(3):
        rt[i * width : (i + 1) * width] = sel
        rt[3 * width + i * COHORTS : 3 * width + (i + 1) * COHORTS] = m3[i]
    rt[3 * width + 3 * COHORTS :] = jnp.zeros((COHORTS, k), BF16)
    lane = lax.broadcasted_iota(jnp.int32, (COHORTS, 128), 1)
    low = lane < width
    for j in range(k // 128):
        pair = sums[:, j * 128 : (j + 1) * 128]
        st_src[2 * j] = jnp.where(low, pair, count)
        st_src[2 * j + 1] = jnp.where(low, pltpu.roll(pair, 64, 1), count)

    pl.semaphore_wait(barrier, len(peers))
    st = [
        remote(st_src.at[var_of(*q)], st_buf.at[i], st_s.at[i], st_r.at[i], (samp, var_of(*q)))
        for i, q in enumerate(VAR)
    ]

    cp_e2 = remote(e_hbm.at[:, pl.ds(other, half)], e_all.at[pl.ds(rows, rows)], e_sem.at[0], e_sem.at[1], sib)
    cp_co2 = remote(co_hbm, co.at[1], e_sem.at[2], e_sem.at[3], sib)
    cp_e = local(e_hbm.at[:, pl.ds(mine, half)], e_all.at[pl.ds(0, rows)], ld.at[4])
    rs = []
    for step, dx in enumerate((2, 1, 3, 0)):
        xo = (x + dx) % NX
        r0 = pl.multiple_of(xo * (2 * blk), 2 * blk)
        f = dot(d[pl.ds(r0, 2 * blk)], w[...]) + dot_t(lt[:, pl.ds(r0, 2 * blk)], rt[...])
        snd[pl.ds(r0, 2 * blk)] = f.astype(BF16)
        if dx == 0:
            own[...] = f
        for dl in (1, 0):
            if dx or dl:
                i = VAR.index((dx, dl))
                to = var_of(dx, dl)
                rs.append(
                    remote(
                        snd.at[pl.ds(pl.multiple_of(to * blk, blk), blk)], rs_buf.at[i], rs_s.at[i], rs_r.at[i],
                        (samp, to),
                    )
                )

    for cp in st:
        cp.wait_recv()
    t = st_src[var]
    for i in range(len(VAR)):
        t = t + st_buf[i]
    t = jnp.where(low, t, count)
    t_src[...] = t
    ycs = [
        remote(t_src, yc_buf.at[i], yc_s.at[i], yc_r.at[i], (samp_of(0, *q), var)) for i, q in enumerate(YC)
    ]
    cp_e.wait()
    e_own = dot(oh, e_all[pl.ds(0, rows)])
    cp_e2.wait_recv()
    cp_co2.wait_recv()
    oh2 = (co[1] == cohorts).astype(F32).astype(BF16)
    e_sib = dot(oh2, e_all[pl.ds(rows, rows)])

    for cp in rs:
        cp.wait_recv()
    at = pl.multiple_of(l * blk, blk)
    s = own[pl.ds(at, blk)]
    for i in range(len(VAR)):
        s = s + rs_buf[i].astype(F32)
    row = pl.multiple_of(var * blk, blk)
    x_all[pl.ds(row, blk)] = s.astype(BF16)
    ag = [
        remote(x_all.at[pl.ds(row, blk)], x_all.at[pl.ds(row, blk)], ag_s.at[i], ag_r.at[i], (samp, var_of(*q)))
        for i, q in enumerate(VAR)
    ]
    sb = [
        remote(x_all.at[pl.ds(row, blk)], x_all.at[pl.ds(pl.multiple_of(rows + row, blk), blk)], sb_s.at[7], sb_r.at[7], sib)
    ]

    for cp in ycs:
        cp.wait_recv()
    t2 = t
    for i in range(len(YC)):
        t2 = t2 + yc_buf[i]
    t2_src[...] = t2
    zs = [
        remote(t2_src, z_buf.at[i], z_s.at[i], z_r.at[i], (samp_of(q, 0, 0), var)) for i, q in enumerate(ZD)
    ]
    for i in range(len(VAR) - 1, -1, -1):
        dx, dl = VAR[i]
        ag[i].wait_recv()
        got = pl.multiple_of(var_of(-dx, -dl) * blk, blk)
        sb.append(
            remote(
                x_all.at[pl.ds(got, blk)], x_all.at[pl.ds(pl.multiple_of(rows + got, blk), blk)], sb_s.at[i], sb_r.at[i], sib
            )
        )
    for cp in zs:
        cp.wait_recv()
    t3 = t2
    for i in range(len(ZD)):
        t3 = t3 + z_buf[i]
    mean = t3 / pltpu.roll(t3, 64, 1)
    d_src[...] = jnp.where(low, t / jnp.maximum(count, 1.0) - mean, 0.0)
    dm[0, var] = d_src[...]
    dms = []
    for i, q in enumerate(VAR):
        for dc in range(NC):
            n = 2 * i + dc
            dms.append(
                remote(d_src, dm.at[dc, var], dm_s.at[n], dm_r.at[n], (samp_of(0, 0, dc), var_of(*q)))
            )
    dms.append(remote(d_src, dm.at[1, var], dm_s.at[14], dm_r.at[14], sib))

    for cp in sb:
        cp.wait_recv()
    cross[...] = dot_t(x_all[...], e_all[...])
    for cp in dms:
        cp.wait_recv()

    def spread_out(i):
        return jnp.concatenate(
            [jnp.where(low, dm[i, 2 * j], pltpu.roll(dm[i, 2 * j + 1], 64, 1)) for j in range(nv // 2)], axis=1
        )

    d_own = spread_out(0)
    d2 = [split2(d_own), split2(spread_out(1))]
    e2 = [split2(e_own), split2(e_sib)]
    left = jnp.concatenate([d2[i][a] for i in range(2) for a in range(2) for b in range(2)], axis=0)
    right = jnp.concatenate([e2[i][b] for i in range(2) for a in range(2) for b in range(2)], axis=0)
    full = cross[...] + dot_t(left, right)
    cross[...] = full
    cb[...] = full.astype(BF16)
    sub = zrows // NY

    def chunk_rows(dest, dy):
        return pl.ds(pl.multiple_of((dest % NZ) * zrows + ((y + dy) % NY) * sub, sub), sub)

    def hop(i, a, t, src):
        return remote(
            src, zx_buf.at[i, a, t], zx_s.at[i, a, t], zx_r.at[i, a, t], (samp_of(1 - 2 * a, 0, 0), var)
        )

    ring = {}
    for i, dy in enumerate(DY):
        for a in range(2):
            n = hops_of(i, a)
            ring[i, a, 0] = hop(i, a, 0, cb.at[chunk_rows(z + (1 - 2 * a) * n + NZ, dy)])

    xo = x_all[pl.ds(0, rows)]
    xf = xo.astype(F32)
    resid = dot(oh, xo)
    q = jnp.sum(xf * xf, axis=0, keepdims=True)
    q = q + jnp.sum(d_own * (2.0 * resid + count * d_own), axis=0, keepdims=True)
    q_src[...] = jnp.concatenate([q[:, j * 128 : (j + 1) * 128] for j in range(k // 128)] * 2, axis=0)
    qy = [
        remote(q_src, q_yc.at[i], qy_s.at[i], qy_r.at[i], (samp_of(0, *a), var)) for i, a in enumerate(YC)
    ]
    yx = {}
    for t in range(1, 5):
        if t == 3:
            for cp in qy:
                cp.wait_recv()
            q2 = q_src[...]
            for i in range(len(YC)):
                q2 = q2 + q_yc[i]
            q2_src[...] = q2
            qz = [
                remote(q2_src, q_z.at[i], qz_s.at[i], qz_r.at[i], (samp_of(b, 0, 0), var))
                for i, b in enumerate(ZD)
            ]
        for i, dy in enumerate(DY):
            for a in range(2):
                n = hops_of(i, a)
                if t >= n:
                    continue
                ring[i, a, t - 1].wait_recv()
                part = zx_buf[i, a, t - 1].astype(F32) + cross[chunk_rows(z + (1 - 2 * a) * (n - t) + NZ, dy)]
                zx_src[i, a, t] = part.astype(BF16)
                ring[i, a, t] = hop(i, a, t, zx_src.at[i, a, t])
            if t == 4:
                acc = cross[chunk_rows(z, dy)]
                for a in range(2):
                    n = hops_of(i, a)
                    ring[i, a, n - 1].wait_recv()
                    acc = acc + zx_buf[i, a, n - 1].astype(F32)
                ysrc[i, 0] = acc[:8]
                ysrc[i, 1] = acc[8:]
                for dc in (1, 0):
                    if dy or dc:
                        m = YC.index((dy, dc))
                        yx[m] = remote(
                            ysrc.at[i, (c + dc) % NC], yx_buf.at[m], yx_s.at[m], yx_r.at[m], (samp_of(0, dy, dc), var)
                        )
    yx = [yx[m] for m in range(len(YC))]
    zx = list(ring.values())
    for cp in qz:
        cp.wait_recv()
    q3 = q2
    for i in range(len(ZD)):
        q3 = q3 + q_z[i]
    spread = lax.rsqrt(q3[:4] / total + 1e-6) / total
    spread = jnp.concatenate([spread[j : j + 1] for j in range(4)], axis=1)
    at_row = lax.broadcasted_iota(jnp.int32, (8, k), 1) - samp * 8 == lax.broadcasted_iota(jnp.int32, (8, k), 0)
    scale = jnp.sum(jnp.where(at_row, spread, 0.0), axis=1, keepdims=True)

    for cp in yx:
        cp.wait_recv()
    same = ysrc[len(DY) - 1, c]
    cross_half = jnp.zeros_like(same)
    for i, (dy, dc) in enumerate(YC):
        if dc:
            cross_half = cross_half + yx_buf[i]
        else:
            same = same + yx_buf[i]
    o_ref[:, pl.ds(mine, half)] = same * scale
    o_ref[:, pl.ds(other, half)] = cross_half * scale

    for cp in [cp_e2, cp_co2] + st + rs + ycs + ag + sb + zs + dms + zx + qy + qz + yx:
        cp.wait_send()


def shards(total, dosages, weights, prior, cohort, expression):
    rows, depth = dosages.shape
    k = weights.shape[1]
    genes = expression.shape[1]
    half = genes // 2
    width = prior.shape[1]
    blk = rows // 8
    out_rows = k // 64
    vm, sem = pltpu.VMEM, pltpu.SemaphoreType.DMA
    scratch = [
        vm((rows, depth), BF16), vm((depth, k), BF16), vm((width, rows), F32), vm((2, 1, rows), jnp.int32),
        vm((2 * rows, half), BF16), vm((3 * width + 4 * COHORTS, rows), BF16), vm((3 * width + 4 * COHORTS, k), BF16),
        vm((rows, k), BF16), vm((2 * blk, k), F32), vm((7, blk, k), BF16), vm((2 * rows, k), BF16),
        vm((8, COHORTS, 128), F32), vm((7, COHORTS, 128), F32), vm((COHORTS, 128), F32), vm((7, COHORTS, 128), F32),
        vm((COHORTS, 128), F32), vm((7, COHORTS, 128), F32),
        vm((COHORTS, 128), F32), vm((2, 8, COHORTS, 128), F32), vm((k, half), F32), vm((k, half), BF16),
        vm((4, 2, 4, k // 32, half), BF16), vm((4, 2, 4, k // 32, half), BF16), vm((4, 2, out_rows, half), F32), vm((7, out_rows, half), F32),
        vm((8, 128), F32), vm((7, 8, 128), F32), vm((8, 128), F32), vm((7, 8, 128), F32),
        sem((5,)), sem((4,)), sem((7,)), sem((7,)), sem((7,)), sem((7,)), sem((7,)), sem((7,)),
        sem((15,)), sem((15,)), sem((7,)), sem((7,)), sem((7,)), sem((7,)), sem((8,)), sem((8,)),
        sem((4, 2, 4)), sem((4, 2, 4)), sem((7,)), sem((7,)), sem((7,)), sem((7,)), sem((7,)), sem((7,)),
    ]
    return pl.pallas_call(
        functools.partial(kernel, float(total)),
        out_shape=jax.ShapeDtypeStruct((out_rows, genes), F32),
        in_specs=[pl.BlockSpec(memory_space=pl.ANY)] * 5,
        out_specs=pl.BlockSpec(memory_space=pltpu.VMEM),
        scratch_shapes=scratch,
        compiler_params=pltpu.CompilerParams(
            collective_id=0, has_side_effects=True, vmem_limit_bytes=67043328
        ),
    )(dosages, weights, prior.T, cohort.reshape(1, rows), expression)


def solution(mesh):
    placed = (P("samp", "var"), P("var", None), P("samp", "var"), P("samp", None), P("samp", "var"))

    def run(dosages, weights, prior, cohort, expression):
        body = functools.partial(shards, dosages.shape[0])
        return jax.shard_map(body, mesh=mesh, in_specs=placed, out_specs=P("samp", "var"), check_vma=False)(
            dosages, weights, prior, cohort, expression
        )

    return run
```

```python
import functools

import jax
import jax.numpy as jnp
from jax import lax
from jax.experimental import pallas as pl
from jax.experimental.pallas import tpu as pltpu
from jax.sharding import PartitionSpec as P

COHORTS = 16
MESH = pl.DeviceIdType.MESH
F32 = jnp.float32
BF16 = jnp.bfloat16
NX, NL, NZ, NY, NC = 4, 2, 8, 4, 2
VAR = [(dx, dl) for dx in (2, 1, 3, 0) for dl in (1, 0) if dx or dl]
YC = [(dy, dc) for dy in (2, 1, 3, 0) for dc in (1, 0) if dy or dc]
ZD = [4, 3, 5, 2, 6, 1, 7]
DY = (2, 1, 3, 0)


def split2(a):
    hi = a.astype(BF16)
    return hi, (a - hi.astype(F32)).astype(BF16)


def split3(a):
    hi = a.astype(BF16)
    rest = a - hi.astype(F32)
    mid = rest.astype(BF16)
    return hi, mid, (rest - mid.astype(F32)).astype(BF16)


def dot(a, b):
    return jnp.dot(a, b, preferred_element_type=F32)


def dot_t(a, b):
    return lax.dot_general(a, b, (((0,), (0,)), ((), ())), preferred_element_type=F32)


def dot_nt(a, b):
    return lax.dot_general(a, b, (((1,), (1,)), ((), ())), preferred_element_type=F32)


def kernel(
    total, d_hbm, w_hbm, p_hbm, co_hbm, e_hbm, o_ref,
    d, w, p, co, e_all, lt, rt, snd, own, rs_buf, x_all, st_src, st_buf, t_src, yc_buf, t2_src, z_buf,
    d_src, dm, cross, cb, zx_buf, zx_src, ysrc, yx_buf, q_src, q_yc, q2_src, q_z,
    ld, e_sem, st_s, st_r, yc_s, yc_r, z_s, z_r, dm_s, dm_r, rs_s, rs_r, ag_s, ag_r, sb_s, sb_r,
    zx_s, zx_r, yx_s, yx_r, qy_s, qy_r, qz_s, qz_r,
):
    samp, var = lax.axis_index("samp"), lax.axis_index("var")
    z, y, c = samp // 8, (samp // 2) % 4, samp % 2
    x, l = var // 2, var % 2
    nv = NX * NL
    rows = d.shape[0]
    blk = rows // nv
    k = w.shape[1]
    half = e_all.shape[1]
    zrows = k // NZ

    def var_of(dx, dl):
        return ((x + dx) % NX) * NL + (l + dl) % NL

    def samp_of(dz, dy, dc):
        return ((z + dz) % NZ) * 8 + ((y + dy) % NY) * 2 + (c + dc) % NC

    sib = (samp_of(0, 0, 1), var)

    def remote(src, dst, ss, rs, dev):
        cp = pltpu.make_async_remote_copy(
            src_ref=src, dst_ref=dst, send_sem=ss, recv_sem=rs, device_id=dev, device_id_type=MESH
        )
        cp.start()
        return cp

    def local(src, dst, sem):
        cp = pltpu.make_async_copy(src, dst, sem)
        cp.start()
        return cp

    barrier = pltpu.get_barrier_semaphore()
    peers = (
        [(samp, var_of(*q)) for q in VAR]
        + [(samp_of(0, 0, 1), var_of(*q)) for q in VAR]
        + [(samp_of(0, *q), var) for q in YC]
        + [(samp_of(q, 0, 0), var) for q in ZD]
    )
    for dev in peers:
        pl.semaphore_signal(barrier, inc=1, device_id=dev, device_id_type=MESH)

    cp_co = local(co_hbm, co.at[0], ld.at[0])
    cp_p = local(p_hbm, p, ld.at[3])
    cp_d = local(d_hbm, d, ld.at[1])
    cp_w = local(w_hbm, w, ld.at[2])
    mine = pl.multiple_of(c * half, 128)
    other = pl.multiple_of((1 - c) * half, 128)

    cp_co.wait()
    cohorts = lax.broadcasted_iota(jnp.int32, (COHORTS, rows), 0)
    hot = (co[0] == cohorts).astype(F32)
    oh = hot.astype(BF16)
    count = jnp.sum(hot, axis=1, keepdims=True)
    cp_p.wait()
    p3 = split3(p[...])
    width = p.shape[0]
    for i in range(3):
        lt[i * width : (i + 1) * width] = p3[i]
        lt[3 * width + i * COHORTS : 3 * width + (i + 1) * COHORTS] = oh
    lt[3 * width + 3 * COHORTS :] = jnp.zeros((COHORTS, rows), BF16)
    sel = lax.broadcasted_iota(jnp.int32, (width, k), 1) - var * width == lax.broadcasted_iota(jnp.int32, (width, k), 0)
    sel = sel.astype(F32).astype(BF16)
    ps = [dot_nt(oh, p3[i]) for i in range(3)]
    ps = ps[0] + ps[1] + ps[2]
    ps = sum(dot(part, sel) for part in split3(ps))
    cp_d.wait()
    a3 = split3(dot(oh, d[...]))
    cp_w.wait()
    sums = ps + sum(dot(part, w[...]) for part in a3)
    m3 = split3(-sums / jnp.maximum(count, 1.0))
    for i in range(3):
        rt[i * width : (i + 1) * width] = sel
        rt[3 * width + i * COHORTS : 3 * width + (i + 1) * COHORTS] = m3[i]
    rt[3 * width + 3 * COHORTS :] = jnp.zeros((COHORTS, k), BF16)
    lane = lax.broadcasted_iota(jnp.int32, (COHORTS, 128), 1)
    low = lane < width
    for j in range(k // 128):
        pair = sums[:, j * 128 : (j + 1) * 128]
        st_src[2 * j] = jnp.where(low, pair, count)
        st_src[2 * j + 1] = jnp.where(low, pltpu.roll(pair, 64, 1), count)

    pl.semaphore_wait(barrier, len(peers))
    st = [
        remote(st_src.at[var_of(*q)], st_buf.at[i], st_s.at[i], st_r.at[i], (samp, var_of(*q)))
        for i, q in enumerate(VAR)
    ]

    cp_e2 = remote(e_hbm.at[:, pl.ds(other, half)], e_all.at[pl.ds(rows, rows)], e_sem.at[0], e_sem.at[1], sib)
    cp_co2 = remote(co_hbm, co.at[1], e_sem.at[2], e_sem.at[3], sib)
    cp_e = local(e_hbm.at[:, pl.ds(mine, half)], e_all.at[pl.ds(0, rows)], ld.at[4])
    hb = blk // 2

    def send_part(q, h):
        i = VAR.index(q)
        to = var_of(*q)
        return remote(
            snd.at[pl.ds(pl.multiple_of(to * blk + h * hb, hb), hb)], rs_buf.at[i, h], rs_s.at[i, h], rs_r.at[i, h], (samp, to)
        )

    rs = {}
    for dx in (2, 1, 3, 0):
        xo = (x + dx) % NX
        r0 = pl.multiple_of(xo * (2 * blk), 2 * blk)
        f = dot(d[pl.ds(r0, 2 * blk)], w[...]) + dot_t(lt[:, pl.ds(r0, 2 * blk)], rt[...])
        snd[pl.ds(r0, 2 * blk)] = f.astype(BF16)
        if dx == 0:
            own[...] = f
        for q in VAR:
            if q[0] == dx:
                rs[q, 0] = send_part(q, 0)
    for q in VAR:
        rs[q, 1] = send_part(q, 1)

    for cp in st:
        cp.wait_recv()
    t = st_src[var]
    for i in range(len(VAR)):
        t = t + st_buf[i]
    t = jnp.where(low, t, count)
    t_src[...] = t
    zs = [
        remote(t_src, z_buf.at[i], z_s.at[i], z_r.at[i], (samp_of(q, 0, 0), var)) for i, q in enumerate(ZD)
    ]
    cp_e.wait()
    e_own = dot(oh, e_all[pl.ds(0, rows)])
    cp_e2.wait_recv()
    cp_co2.wait_recv()
    oh2 = (co[1] == cohorts).astype(F32).astype(BF16)
    e_sib = dot(oh2, e_all[pl.ds(rows, rows)])

    ag, sb = {}, {}

    def spread_part(h):
        for q in VAR:
            rs[q, h].wait_recv()
        s = own[pl.ds(pl.multiple_of(l * blk + h * hb, hb), hb)]
        for i in range(len(VAR)):
            s = s + rs_buf[i, h].astype(F32)
        row = pl.multiple_of(var * blk + h * hb, hb)
        x_all[pl.ds(row, hb)] = s.astype(BF16)
        for i, q in enumerate(VAR):
            ag[i, h] = remote(
                x_all.at[pl.ds(row, hb)], x_all.at[pl.ds(row, hb)], ag_s.at[i, h], ag_r.at[i, h], (samp, var_of(*q))
            )
        sb[7, h] = share(7, h, row)

    def share(i, h, row):
        return remote(
            x_all.at[pl.ds(row, hb)], x_all.at[pl.ds(pl.multiple_of(rows + row, hb), hb)], sb_s.at[i, h], sb_r.at[i, h], sib
        )

    spread_part(0)
    for cp in zs:
        cp.wait_recv()
    t2 = t
    for i in range(len(ZD)):
        t2 = t2 + z_buf[i]
    t2_src[...] = t2
    ycs = [
        remote(t2_src, yc_buf.at[i], yc_s.at[i], yc_r.at[i], (samp_of(0, *q), var)) for i, q in enumerate(YC)
    ]
    spread_part(1)

    def pass_on(h):
        for i in range(len(VAR) - 1, -1, -1):
            dx, dl = VAR[i]
            ag[i, h].wait_recv()
            sb[i, h] = share(i, h, pl.multiple_of(var_of(-dx, -dl) * blk + h * hb, hb))

    pass_on(0)
    for cp in ycs:
        cp.wait_recv()
    t3 = t2
    for i in range(len(YC)):
        t3 = t3 + yc_buf[i]
    mean = t3 / pltpu.roll(t3, 64, 1)
    d_src[...] = jnp.where(low, t / jnp.maximum(count, 1.0) - mean, 0.0)
    dm[0, var] = d_src[...]
    dms = []
    for i, q in enumerate(VAR):
        for dc in range(NC):
            n = 2 * i + dc
            dms.append(
                remote(d_src, dm.at[dc, var], dm_s.at[n], dm_r.at[n], (samp_of(0, 0, dc), var_of(*q)))
            )
    dms.append(remote(d_src, dm.at[1, var], dm_s.at[14], dm_r.at[14], sib))

    pass_on(1)
    for cp in sb.values():
        cp.wait_recv()
    cross[...] = dot_t(x_all[...], e_all[...])
    for cp in dms:
        cp.wait_recv()

    def spread_out(i):
        return jnp.concatenate(
            [jnp.where(low, dm[i, 2 * j], pltpu.roll(dm[i, 2 * j + 1], 64, 1)) for j in range(nv // 2)], axis=1
        )

    d_own = spread_out(0)
    d2 = [split2(d_own), split2(spread_out(1))]
    e2 = [split2(e_own), split2(e_sib)]
    left = jnp.concatenate([d2[i][a] for i in range(2) for a in range(2) for b in range(2)], axis=0)
    right = jnp.concatenate([e2[i][b] for i in range(2) for a in range(2) for b in range(2)], axis=0)
    full = cross[...] + dot_t(left, right)
    cross[...] = full
    cb[...] = full.astype(BF16)
    sub = zrows // NY

    def chunk_rows(dest, dy):
        return pl.ds(pl.multiple_of((dest % NZ) * zrows + ((y + dy) % NY) * sub, sub), sub)

    def hop(i, n, to, src):
        return remote(
            src, zx_buf.at[i, n], zx_s.at[i, n], zx_r.at[i, n], (samp_of(to, 0, 0), var)
        )

    zx = {}
    for i, dy in enumerate(DY):
        turn = 1 if i % 2 == 0 else -1
        zx[i, 0] = hop(i, 0, 2 * turn, cb.at[chunk_rows(z + 4, dy)])
        zx[i, 1] = hop(i, 1, 1, cb.at[chunk_rows(z + 3, dy)])
        zx[i, 2] = hop(i, 2, -1, cb.at[chunk_rows(z + NZ - 3, dy)])
    for i, dy in enumerate(DY):
        zx[i, 5] = hop(i, 5, 1, cb.at[chunk_rows(z + 1, dy)])
        zx[i, 6] = hop(i, 6, -1, cb.at[chunk_rows(z + NZ - 1, dy)])

    xo = x_all[pl.ds(0, rows)]
    xf = xo.astype(F32)
    resid = dot(oh, xo)
    q = jnp.sum(xf * xf, axis=0, keepdims=True)
    q = q + jnp.sum(d_own * (2.0 * resid + count * d_own), axis=0, keepdims=True)
    q_src[...] = jnp.concatenate([q[:, j * 128 : (j + 1) * 128] for j in range(k // 128)] * 2, axis=0)
    qy = [
        remote(q_src, q_yc.at[i], qy_s.at[i], qy_r.at[i], (samp_of(0, *a), var)) for i, a in enumerate(YC)
    ]
    for i, dy in enumerate(DY):
        turn = 1 if i % 2 == 0 else -1
        for n in range(3):
            zx[i, n].wait_recv()
        for a, way in enumerate((1, -1)):
            part = cross[chunk_rows(z + 2 * way + NZ, dy)] + zx_buf[i, 1 + a].astype(F32)
            if way == turn:
                part = part + zx_buf[i, 0].astype(F32)
            zx_src[i, a] = part.astype(BF16)
            zx[i, 3 + a] = hop(i, 3 + a, 2 * way, zx_src.at[i, a])
    for cp in qy:
        cp.wait_recv()
    q2 = q_src[...]
    for i in range(len(YC)):
        q2 = q2 + q_yc[i]
    q2_src[...] = q2
    qz = [
        remote(q2_src, q_z.at[i], qz_s.at[i], qz_r.at[i], (samp_of(b, 0, 0), var)) for i, b in enumerate(ZD)
    ]
    yx = {}
    for i, dy in enumerate(DY):
        acc = cross[chunk_rows(z, dy)]
        for n in (5, 6, 3, 4):
            zx[i, n].wait_recv()
            acc = acc + zx_buf[i, n].astype(F32)
        ysrc[i, 0] = acc[:8]
        ysrc[i, 1] = acc[8:]
        for dc in (1, 0):
            if dy or dc:
                m = YC.index((dy, dc))
                yx[m] = remote(
                    ysrc.at[i, (c + dc) % NC], yx_buf.at[m], yx_s.at[m], yx_r.at[m], (samp_of(0, dy, dc), var)
                )
    yx = [yx[m] for m in range(len(YC))]
    zx, rs, ag, sb = [list(group.values()) for group in (zx, rs, ag, sb)]
    for cp in qz:
        cp.wait_recv()
    q3 = q2
    for i in range(len(ZD)):
        q3 = q3 + q_z[i]
    spread = lax.rsqrt(q3[:4] / total + 1e-6) / total
    spread = jnp.concatenate([spread[j : j + 1] for j in range(4)], axis=1)
    at_row = lax.broadcasted_iota(jnp.int32, (8, k), 1) - samp * 8 == lax.broadcasted_iota(jnp.int32, (8, k), 0)
    scale = jnp.sum(jnp.where(at_row, spread, 0.0), axis=1, keepdims=True)

    for cp in yx:
        cp.wait_recv()
    same = ysrc[len(DY) - 1, c]
    cross_half = jnp.zeros_like(same)
    for i, (dy, dc) in enumerate(YC):
        if dc:
            cross_half = cross_half + yx_buf[i]
        else:
            same = same + yx_buf[i]
    o_ref[:, pl.ds(mine, half)] = same * scale
    o_ref[:, pl.ds(other, half)] = cross_half * scale

    for cp in [cp_e2, cp_co2] + st + rs + ycs + ag + sb + zs + dms + zx + qy + qz + yx:
        cp.wait_send()


def shards(total, dosages, weights, prior, cohort, expression):
    rows, depth = dosages.shape
    k = weights.shape[1]
    genes = expression.shape[1]
    half = genes // 2
    width = prior.shape[1]
    blk = rows // 8
    out_rows = k // 64
    vm, sem = pltpu.VMEM, pltpu.SemaphoreType.DMA
    scratch = [
        vm((rows, depth), BF16), vm((depth, k), BF16), vm((width, rows), F32), vm((2, 1, rows), jnp.int32),
        vm((2 * rows, half), BF16), vm((3 * width + 4 * COHORTS, rows), BF16), vm((3 * width + 4 * COHORTS, k), BF16),
        vm((rows, k), BF16), vm((2 * blk, k), F32), vm((7, 2, blk // 2, k), BF16), vm((2 * rows, k), BF16),
        vm((8, COHORTS, 128), F32), vm((7, COHORTS, 128), F32), vm((COHORTS, 128), F32), vm((7, COHORTS, 128), F32),
        vm((COHORTS, 128), F32), vm((7, COHORTS, 128), F32),
        vm((COHORTS, 128), F32), vm((2, 8, COHORTS, 128), F32), vm((k, half), F32), vm((k, half), BF16),
        vm((4, 7, k // 32, half), BF16), vm((4, 2, k // 32, half), BF16), vm((4, 2, out_rows, half), F32), vm((7, out_rows, half), F32),
        vm((8, 128), F32), vm((7, 8, 128), F32), vm((8, 128), F32), vm((7, 8, 128), F32),
        sem((5,)), sem((4,)), sem((7,)), sem((7,)), sem((7,)), sem((7,)), sem((7,)), sem((7,)),
        sem((15,)), sem((15,)), sem((7, 2)), sem((7, 2)), sem((7, 2)), sem((7, 2)), sem((8, 2)), sem((8, 2)),
        sem((4, 7)), sem((4, 7)), sem((7,)), sem((7,)), sem((7,)), sem((7,)), sem((7,)), sem((7,)),
    ]
    return pl.pallas_call(
        functools.partial(kernel, float(total)),
        out_shape=jax.ShapeDtypeStruct((out_rows, genes), F32),
        in_specs=[pl.BlockSpec(memory_space=pl.ANY)] * 5,
        out_specs=pl.BlockSpec(memory_space=pltpu.VMEM),
        scratch_shapes=scratch,
        compiler_params=pltpu.CompilerParams(
            collective_id=0, has_side_effects=True, vmem_limit_bytes=67043328
        ),
    )(dosages, weights, prior.T, cohort.reshape(1, rows), expression)


def solution(mesh):
    placed = (P("samp", "var"), P("var", None), P("samp", "var"), P("samp", None), P("samp", "var"))

    def run(dosages, weights, prior, cohort, expression):
        body = functools.partial(shards, dosages.shape[0])
        return jax.shard_map(body, mesh=mesh, in_specs=placed, out_specs=P("samp", "var"), check_vma=False)(
            dosages, weights, prior, cohort, expression
        )

    return run
```

```python
import functools

import jax
import jax.numpy as jnp
from jax import lax
from jax.experimental import pallas as pl
from jax.experimental.pallas import tpu as pltpu
from jax.sharding import PartitionSpec as P

COHORTS = 16
MESH = pl.DeviceIdType.MESH
F32 = jnp.float32
BF16 = jnp.bfloat16
NX, NL, NZ, NY, NC = 4, 2, 8, 4, 2
VAR = [(dx, dl) for dx in (2, 1, 3, 0) for dl in (1, 0) if dx or dl]
YC = [(dy, dc) for dy in (2, 1, 3, 0) for dc in (1, 0) if dy or dc]
ZD = [4, 3, 5, 2, 6, 1, 7]
DY = (2, 1, 3, 0)


def split2(a):
    hi = a.astype(BF16)
    return hi, (a - hi.astype(F32)).astype(BF16)


def split3(a):
    hi = a.astype(BF16)
    rest = a - hi.astype(F32)
    mid = rest.astype(BF16)
    return hi, mid, (rest - mid.astype(F32)).astype(BF16)


def dot(a, b):
    return jnp.dot(a, b, preferred_element_type=F32)


def dot_t(a, b):
    return lax.dot_general(a, b, (((0,), (0,)), ((), ())), preferred_element_type=F32)


def dot_nt(a, b):
    return lax.dot_general(a, b, (((1,), (1,)), ((), ())), preferred_element_type=F32)


def kernel(
    total, d_hbm, w_hbm, p_hbm, co_hbm, e_hbm, o_ref,
    d, w, p, co, e_all, lt, rt, snd, own, rs_buf, x_all, st_src, st_buf, t_src, yc_buf, t2_src, z_buf,
    d_src, dm, cross, cb, zx_buf, zx_src, own_y, ysrc, yx_buf, q_src, q_yc, q2_src, q_z,
    ld, e_sem, st_s, st_r, yc_s, yc_r, z_s, z_r, dm_s, dm_r, rs_s, rs_r, ag_s, ag_r, sb_s, sb_r,
    zx_s, zx_r, yx_s, yx_r, qy_s, qy_r, qz_s, qz_r,
):
    samp, var = lax.axis_index("samp"), lax.axis_index("var")
    z, y, c = samp // 8, (samp // 2) % 4, samp % 2
    x, l = var // 2, var % 2
    nv = NX * NL
    rows = d.shape[0]
    blk = rows // nv
    k = w.shape[1]
    half = e_all.shape[1]
    zrows = k // NZ

    def var_of(dx, dl):
        return ((x + dx) % NX) * NL + (l + dl) % NL

    def samp_of(dz, dy, dc):
        return ((z + dz) % NZ) * 8 + ((y + dy) % NY) * 2 + (c + dc) % NC

    sib = (samp_of(0, 0, 1), var)

    def remote(src, dst, ss, rs, dev):
        cp = pltpu.make_async_remote_copy(
            src_ref=src, dst_ref=dst, send_sem=ss, recv_sem=rs, device_id=dev, device_id_type=MESH
        )
        cp.start()
        return cp

    def local(src, dst, sem):
        cp = pltpu.make_async_copy(src, dst, sem)
        cp.start()
        return cp

    barrier = pltpu.get_barrier_semaphore()
    peers = (
        [(samp, var_of(*q)) for q in VAR]
        + [(samp_of(0, 0, 1), var_of(*q)) for q in VAR]
        + [(samp_of(0, *q), var) for q in YC]
        + [(samp_of(q, 0, 0), var) for q in ZD]
    )
    for dev in peers:
        pl.semaphore_signal(barrier, inc=1, device_id=dev, device_id_type=MESH)

    cp_co = local(co_hbm, co.at[0], ld.at[0])
    cp_p = local(p_hbm, p, ld.at[3])
    cp_d = local(d_hbm, d, ld.at[1])
    cp_w = local(w_hbm, w, ld.at[2])
    mine = pl.multiple_of(c * half, 128)
    other = pl.multiple_of((1 - c) * half, 128)

    cp_co.wait()
    cohorts = lax.broadcasted_iota(jnp.int32, (COHORTS, rows), 0)
    hot = (co[0] == cohorts).astype(F32)
    oh = hot.astype(BF16)
    count = jnp.sum(hot, axis=1, keepdims=True)
    cp_p.wait()
    p3 = split3(p[...])
    width = p.shape[0]
    for i in range(3):
        lt[i * width : (i + 1) * width] = p3[i]
        lt[3 * width + i * COHORTS : 3 * width + (i + 1) * COHORTS] = oh
    lt[3 * width + 3 * COHORTS :] = jnp.zeros((COHORTS, rows), BF16)
    sel = lax.broadcasted_iota(jnp.int32, (width, k), 1) - var * width == lax.broadcasted_iota(jnp.int32, (width, k), 0)
    sel = sel.astype(F32).astype(BF16)
    ps = [dot_nt(oh, p3[i]) for i in range(3)]
    ps = ps[0] + ps[1] + ps[2]
    ps = sum(dot(part, sel) for part in split3(ps))
    cp_d.wait()
    a3 = split3(dot(oh, d[...]))
    cp_w.wait()
    sums = ps + sum(dot(part, w[...]) for part in a3)
    m3 = split3(-sums / jnp.maximum(count, 1.0))
    for i in range(3):
        rt[i * width : (i + 1) * width] = sel
        rt[3 * width + i * COHORTS : 3 * width + (i + 1) * COHORTS] = m3[i]
    rt[3 * width + 3 * COHORTS :] = jnp.zeros((COHORTS, k), BF16)
    lane = lax.broadcasted_iota(jnp.int32, (COHORTS, 128), 1)
    low = lane < width
    for j in range(k // 128):
        pair = sums[:, j * 128 : (j + 1) * 128]
        st_src[2 * j] = jnp.where(low, pair, count)
        st_src[2 * j + 1] = jnp.where(low, pltpu.roll(pair, 64, 1), count)

    pl.semaphore_wait(barrier, len(peers))
    st = [
        remote(st_src.at[var_of(*q)], st_buf.at[i], st_s.at[i], st_r.at[i], (samp, var_of(*q)))
        for i, q in enumerate(VAR)
    ]

    cp_e2 = remote(e_hbm.at[:, pl.ds(other, half)], e_all.at[pl.ds(rows, rows)], e_sem.at[0], e_sem.at[1], sib)
    cp_co2 = remote(co_hbm, co.at[1], e_sem.at[2], e_sem.at[3], sib)
    cp_e = local(e_hbm.at[:, pl.ds(mine, half)], e_all.at[pl.ds(0, rows)], ld.at[4])
    hb = blk // 2
    hr = rows // 2

    def product(h):
        f = dot(d[h * hr : (h + 1) * hr], w[...]) + dot_t(lt[:, h * hr : (h + 1) * hr], rt[...])
        snd[h] = f.astype(BF16)
        own[h] = f

    def send_parts(h):
        for i, q in enumerate(VAR):
            to = var_of(*q)
            rs[q, h] = remote(
                snd.at[h, pl.ds(pl.multiple_of(to * hb, hb), hb)], rs_buf.at[i, h], rs_s.at[i, h], rs_r.at[i, h], (samp, to)
            )

    rs = {}
    product(0)
    send_parts(0)
    product(1)
    for cp in st:
        cp.wait_recv()
    t = st_src[var]
    for i in range(len(VAR)):
        t = t + st_buf[i]
    t = jnp.where(low, t, count)
    t_src[...] = t
    zs = [
        remote(t_src, z_buf.at[i], z_s.at[i], z_r.at[i], (samp_of(q, 0, 0), var)) for i, q in enumerate(ZD)
    ]
    send_parts(1)
    cp_e.wait()
    e_own = dot(oh, e_all[pl.ds(0, rows)])
    cp_e2.wait_recv()
    cp_co2.wait_recv()
    oh2 = (co[1] == cohorts).astype(F32).astype(BF16)
    e_sib = dot(oh2, e_all[pl.ds(rows, rows)])

    ag, sb = {}, {}

    def spread_part(h):
        for q in VAR:
            rs[q, h].wait_recv()
        s = own[h, pl.ds(pl.multiple_of(var * hb, hb), hb)]
        for i in range(len(VAR)):
            s = s + rs_buf[i, h].astype(F32)
        row = pl.multiple_of(h * hr + var * hb, hb)
        x_all[pl.ds(row, hb)] = s.astype(BF16)
        for i, q in enumerate(VAR):
            ag[i, h] = remote(
                x_all.at[pl.ds(row, hb)], x_all.at[pl.ds(row, hb)], ag_s.at[i, h], ag_r.at[i, h], (samp, var_of(*q))
            )
        sb[7, h] = share(7, h, row)

    def share(i, h, row):
        return remote(
            x_all.at[pl.ds(row, hb)], x_all.at[pl.ds(pl.multiple_of(rows + row, hb), hb)], sb_s.at[i, h], sb_r.at[i, h], sib
        )

    spread_part(0)
    for cp in zs:
        cp.wait_recv()
    t2 = t
    for i in range(len(ZD)):
        t2 = t2 + z_buf[i]
    t2_src[...] = t2
    ycs = [
        remote(t2_src, yc_buf.at[i], yc_s.at[i], yc_r.at[i], (samp_of(0, *q), var)) for i, q in enumerate(YC)
    ]
    spread_part(1)

    def pass_on(h):
        for i in range(len(VAR) - 1, -1, -1):
            dx, dl = VAR[i]
            ag[i, h].wait_recv()
            sb[i, h] = share(i, h, pl.multiple_of(h * hr + var_of(-dx, -dl) * hb, hb))

    def multiply(h):
        own_half = dot_t(x_all[h * hr : (h + 1) * hr], e_all[h * hr : (h + 1) * hr])
        for i in range(8):
            sb[i, h].wait_recv()
        lo = rows + h * hr
        return own_half + dot_t(x_all[lo : lo + hr], e_all[lo : lo + hr])

    pass_on(0)
    for cp in ycs:
        cp.wait_recv()
    t3 = t2
    for i in range(len(YC)):
        t3 = t3 + yc_buf[i]
    mean = t3 / pltpu.roll(t3, 64, 1)
    d_src[...] = jnp.where(low, t / jnp.maximum(count, 1.0) - mean, 0.0)
    dm[0, var] = d_src[...]
    dms = []
    for i, q in enumerate(VAR):
        for dc in range(NC):
            n = 2 * i + dc
            dms.append(
                remote(d_src, dm.at[dc, var], dm_s.at[n], dm_r.at[n], (samp_of(0, 0, dc), var_of(*q)))
            )
    dms.append(remote(d_src, dm.at[1, var], dm_s.at[14], dm_r.at[14], sib))

    cross[...] = multiply(0)
    pass_on(1)
    cross[...] += multiply(1)
    for cp in dms:
        cp.wait_recv()

    def spread_out(i):
        return jnp.concatenate(
            [jnp.where(low, dm[i, 2 * j], pltpu.roll(dm[i, 2 * j + 1], 64, 1)) for j in range(nv // 2)], axis=1
        )

    d_own = spread_out(0)
    d2 = [split2(d_own), split2(spread_out(1))]
    e2 = [split2(e_own), split2(e_sib)]
    left = jnp.concatenate([d2[i][a] for i in range(2) for a in range(2) for b in range(2)], axis=0)
    right = jnp.concatenate([e2[i][b] for i in range(2) for a in range(2) for b in range(2)], axis=0)
    full = cross[...] + dot_t(left, right)
    cross[...] = full
    cb[...] = full.astype(BF16)
    sub = zrows // NY

    def chunk_rows(dest, dy):
        return pl.ds(pl.multiple_of((dest % NZ) * zrows + ((y + dy) % NY) * sub, sub), sub)

    def hop(i, n, to, src):
        return remote(
            src, zx_buf.at[i, n], zx_s.at[i, n], zx_r.at[i, n], (samp_of(to, 0, 0), var)
        )

    zx = {}
    for i, dy in enumerate(DY):
        turn = 1 if i % 2 == 0 else -1
        zx[i, 0] = hop(i, 0, 2 * turn, cb.at[chunk_rows(z + 4, dy)])
        zx[i, 1] = hop(i, 1, 1, cb.at[chunk_rows(z + 3, dy)])
        zx[i, 2] = hop(i, 2, -1, cb.at[chunk_rows(z + NZ - 3, dy)])
    for i, dy in enumerate(DY):
        zx[i, 5] = hop(i, 5, 1, cb.at[chunk_rows(z + 1, dy)])
        zx[i, 6] = hop(i, 6, -1, cb.at[chunk_rows(z + NZ - 1, dy)])

    xo = x_all[pl.ds(0, rows)]
    xf = xo.astype(F32)
    resid = dot(oh, xo)
    q = jnp.sum(xf * xf, axis=0, keepdims=True)
    q = q + jnp.sum(d_own * (2.0 * resid + count * d_own), axis=0, keepdims=True)
    q_src[...] = jnp.concatenate([q[:, j * 128 : (j + 1) * 128] for j in range(k // 128)] * 2, axis=0)
    qy = [
        remote(q_src, q_yc.at[i], qy_s.at[i], qy_r.at[i], (samp_of(0, *a), var)) for i, a in enumerate(YC)
    ]
    for i, dy in enumerate(DY):
        turn = 1 if i % 2 == 0 else -1
        for n in range(3):
            zx[i, n].wait_recv()
        for a, way in enumerate((1, -1)):
            part = cross[chunk_rows(z + 2 * way + NZ, dy)] + zx_buf[i, 1 + a].astype(F32)
            if way == turn:
                part = part + zx_buf[i, 0].astype(F32)
            zx_src[i, a] = part.astype(BF16)
            zx[i, 3 + a] = hop(i, 3 + a, 2 * way, zx_src.at[i, a])
    for cp in qy:
        cp.wait_recv()
    q2 = q_src[...]
    for i in range(len(YC)):
        q2 = q2 + q_yc[i]
    q2_src[...] = q2
    qz = [
        remote(q2_src, q_z.at[i], qz_s.at[i], qz_r.at[i], (samp_of(b, 0, 0), var)) for i, b in enumerate(ZD)
    ]
    yx = {}
    for i, dy in enumerate(DY):
        acc = cross[chunk_rows(z, dy)]
        for n in (5, 6, 3, 4):
            zx[i, n].wait_recv()
            acc = acc + zx_buf[i, n].astype(F32)
        if dy == 0:
            own_y[0] = acc[:8]
            own_y[1] = acc[8:]
        ysrc[i, 0] = acc[:8].astype(BF16)
        ysrc[i, 1] = acc[8:].astype(BF16)
        for dc in (1, 0):
            if dy or dc:
                m = YC.index((dy, dc))
                yx[m] = remote(
                    ysrc.at[i, (c + dc) % NC], yx_buf.at[m], yx_s.at[m], yx_r.at[m], (samp_of(0, dy, dc), var)
                )
    yx = [yx[m] for m in range(len(YC))]
    zx, rs, ag, sb = [list(group.values()) for group in (zx, rs, ag, sb)]
    for cp in qz:
        cp.wait_recv()
    q3 = q2
    for i in range(len(ZD)):
        q3 = q3 + q_z[i]
    spread = lax.rsqrt(q3[:4] / total + 1e-6) / total
    spread = jnp.concatenate([spread[j : j + 1] for j in range(4)], axis=1)
    at_row = lax.broadcasted_iota(jnp.int32, (8, k), 1) - samp * 8 == lax.broadcasted_iota(jnp.int32, (8, k), 0)
    scale = jnp.sum(jnp.where(at_row, spread, 0.0), axis=1, keepdims=True)

    for cp in yx:
        cp.wait_recv()
    same = own_y[c]
    cross_half = jnp.zeros_like(same)
    for i, (dy, dc) in enumerate(YC):
        if dc:
            cross_half = cross_half + yx_buf[i].astype(F32)
        else:
            same = same + yx_buf[i].astype(F32)
    o_ref[:, pl.ds(mine, half)] = same * scale
    o_ref[:, pl.ds(other, half)] = cross_half * scale

    for cp in [cp_e2, cp_co2] + st + rs + ycs + ag + sb + zs + dms + zx + qy + qz + yx:
        cp.wait_send()


def shards(total, dosages, weights, prior, cohort, expression):
    rows, depth = dosages.shape
    k = weights.shape[1]
    genes = expression.shape[1]
    half = genes // 2
    width = prior.shape[1]
    blk = rows // 8
    out_rows = k // 64
    vm, sem = pltpu.VMEM, pltpu.SemaphoreType.DMA
    scratch = [
        vm((rows, depth), BF16), vm((depth, k), BF16), vm((width, rows), F32), vm((2, 1, rows), jnp.int32),
        vm((2 * rows, half), BF16), vm((3 * width + 4 * COHORTS, rows), BF16), vm((3 * width + 4 * COHORTS, k), BF16),
        vm((2, rows // 2, k), BF16), vm((2, rows // 2, k), F32), vm((7, 2, blk // 2, k), BF16), vm((2 * rows, k), BF16),
        vm((8, COHORTS, 128), F32), vm((7, COHORTS, 128), F32), vm((COHORTS, 128), F32), vm((7, COHORTS, 128), F32),
        vm((COHORTS, 128), F32), vm((7, COHORTS, 128), F32),
        vm((COHORTS, 128), F32), vm((2, 8, COHORTS, 128), F32), vm((k, half), F32), vm((k, half), BF16),
        vm((4, 7, k // 32, half), BF16), vm((4, 2, k // 32, half), BF16), vm((2, out_rows, half), F32), vm((4, 2, out_rows, half), BF16), vm((7, out_rows, half), BF16),
        vm((8, 128), F32), vm((7, 8, 128), F32), vm((8, 128), F32), vm((7, 8, 128), F32),
        sem((5,)), sem((4,)), sem((7,)), sem((7,)), sem((7,)), sem((7,)), sem((7,)), sem((7,)),
        sem((15,)), sem((15,)), sem((7, 2)), sem((7, 2)), sem((7, 2)), sem((7, 2)), sem((8, 2)), sem((8, 2)),
        sem((4, 7)), sem((4, 7)), sem((7,)), sem((7,)), sem((7,)), sem((7,)), sem((7,)), sem((7,)),
    ]
    return pl.pallas_call(
        functools.partial(kernel, float(total)),
        out_shape=jax.ShapeDtypeStruct((out_rows, genes), F32),
        in_specs=[pl.BlockSpec(memory_space=pl.ANY)] * 5,
        out_specs=pl.BlockSpec(memory_space=pltpu.VMEM),
        scratch_shapes=scratch,
        compiler_params=pltpu.CompilerParams(
            collective_id=0, has_side_effects=True, vmem_limit_bytes=67043328
        ),
    )(dosages, weights, prior.T, cohort.reshape(1, rows), expression)


def solution(mesh):
    placed = (P("samp", "var"), P("var", None), P("samp", "var"), P("samp", None), P("samp", "var"))

    def run(dosages, weights, prior, cohort, expression):
        body = functools.partial(shards, dosages.shape[0])
        return jax.shard_map(body, mesh=mesh, in_specs=placed, out_specs=P("samp", "var"), check_vma=False)(
            dosages, weights, prior, cohort, expression
        )

    return run
```

```python
import functools

import jax
import jax.numpy as jnp
from jax import lax
from jax.experimental import pallas as pl
from jax.experimental.pallas import tpu as pltpu
from jax.sharding import PartitionSpec as P

COHORTS = 16
MESH = pl.DeviceIdType.MESH
F32 = jnp.float32
BF16 = jnp.bfloat16
NX, NL, NZ, NY, NC = 4, 2, 8, 4, 2
VAR = [(dx, dl) for dx in (2, 1, 3, 0) for dl in (1, 0) if dx or dl]
YC = [(dy, dc) for dy in (2, 1, 3, 0) for dc in (1, 0) if dy or dc]
ZD = [4, 3, 5, 2, 6, 1, 7]
DY = (2, 1, 3, 0)


def split2(a):
    hi = a.astype(BF16)
    return hi, (a - hi.astype(F32)).astype(BF16)


def split3(a):
    hi = a.astype(BF16)
    rest = a - hi.astype(F32)
    mid = rest.astype(BF16)
    return hi, mid, (rest - mid.astype(F32)).astype(BF16)


def dot(a, b):
    return jnp.dot(a, b, preferred_element_type=F32)


def dot_t(a, b):
    return lax.dot_general(a, b, (((0,), (0,)), ((), ())), preferred_element_type=F32)


def dot_nt(a, b):
    return lax.dot_general(a, b, (((1,), (1,)), ((), ())), preferred_element_type=F32)


def kernel(
    total, d_hbm, w_hbm, p_hbm, co_hbm, e_hbm, o_ref,
    d, w, p, co, e_all, lt, rt, snd, own, rs_buf, x_all, st_src, st_buf, t_src, yc_buf, t2_src, z_buf,
    d_src, dm, cross, cb, zx_buf, zx_src, own_y, ysrc, yx_buf, q_src, q_yc, q2_src, q_z,
    ld, e_sem, st_s, st_r, yc_s, yc_r, z_s, z_r, dm_s, dm_r, rs_s, rs_r, ag_s, ag_r, sb_s, sb_r,
    zx_s, zx_r, yx_s, yx_r, qy_s, qy_r, qz_s, qz_r,
):
    samp, var = lax.axis_index("samp"), lax.axis_index("var")
    z, y, c = samp // 8, (samp // 2) % 4, samp % 2
    x, l = var // 2, var % 2
    nv = NX * NL
    rows = d.shape[0]
    blk = rows // nv
    k = w.shape[1]
    half = e_all.shape[1]
    zrows = k // NZ

    def var_of(dx, dl):
        return ((x + dx) % NX) * NL + (l + dl) % NL

    def samp_of(dz, dy, dc):
        return ((z + dz) % NZ) * 8 + ((y + dy) % NY) * 2 + (c + dc) % NC

    sib = (samp_of(0, 0, 1), var)

    def remote(src, dst, ss, rs, dev):
        cp = pltpu.make_async_remote_copy(
            src_ref=src, dst_ref=dst, send_sem=ss, recv_sem=rs, device_id=dev, device_id_type=MESH
        )
        cp.start()
        return cp

    def local(src, dst, sem):
        cp = pltpu.make_async_copy(src, dst, sem)
        cp.start()
        return cp

    barrier = pltpu.get_barrier_semaphore()
    peers = (
        [(samp, var_of(*q)) for q in VAR]
        + [(samp_of(0, 0, 1), var_of(*q)) for q in VAR]
        + [(samp_of(0, *q), var) for q in YC]
        + [(samp_of(q, 0, 0), var) for q in ZD]
    )
    for dev in peers:
        pl.semaphore_signal(barrier, inc=1, device_id=dev, device_id_type=MESH)

    cp_co = local(co_hbm, co.at[0], ld.at[0])
    cp_p = local(p_hbm, p, ld.at[3])
    cp_d = local(d_hbm, d, ld.at[1])
    cp_w = local(w_hbm, w, ld.at[2])
    mine = pl.multiple_of(c * half, 128)
    other = pl.multiple_of((1 - c) * half, 128)

    cp_co.wait()
    cohorts = lax.broadcasted_iota(jnp.int32, (COHORTS, rows), 0)
    hot = (co[0] == cohorts).astype(F32)
    oh = hot.astype(BF16)
    count = jnp.sum(hot, axis=1, keepdims=True)
    cp_p.wait()
    p3 = split3(p[...])
    width = p.shape[0]
    for i in range(3):
        lt[i * width : (i + 1) * width] = p3[i]
        lt[3 * width + i * COHORTS : 3 * width + (i + 1) * COHORTS] = oh
    lt[3 * width + 3 * COHORTS :] = jnp.zeros((COHORTS, rows), BF16)
    sel = lax.broadcasted_iota(jnp.int32, (width, k), 1) - var * width == lax.broadcasted_iota(jnp.int32, (width, k), 0)
    sel = sel.astype(F32).astype(BF16)
    ps = [dot_nt(oh, p3[i]) for i in range(3)]
    ps = ps[0] + ps[1] + ps[2]
    ps = sum(dot(part, sel) for part in split3(ps))
    cp_d.wait()
    a3 = split3(dot(oh, d[...]))
    cp_w.wait()
    sums = ps + sum(dot(part, w[...]) for part in a3)
    m3 = split3(-sums / jnp.maximum(count, 1.0))
    for i in range(3):
        rt[i * width : (i + 1) * width] = sel
        rt[3 * width + i * COHORTS : 3 * width + (i + 1) * COHORTS] = m3[i]
    rt[3 * width + 3 * COHORTS :] = jnp.zeros((COHORTS, k), BF16)
    lane = lax.broadcasted_iota(jnp.int32, (COHORTS, 128), 1)
    low = lane < width
    for j in range(k // 128):
        pair = sums[:, j * 128 : (j + 1) * 128]
        st_src[2 * j] = jnp.where(low, pair, count)
        st_src[2 * j + 1] = jnp.where(low, pltpu.roll(pair, 64, 1), count)

    pl.semaphore_wait(barrier, len(peers))
    st = [
        remote(st_src.at[var_of(*q)], st_buf.at[i], st_s.at[i], st_r.at[i], (samp, var_of(*q)))
        for i, q in enumerate(VAR)
    ]

    cp_e2 = remote(e_hbm.at[:, pl.ds(other, half)], e_all.at[pl.ds(rows, rows)], e_sem.at[0], e_sem.at[1], sib)
    cp_co2 = remote(co_hbm, co.at[1], e_sem.at[2], e_sem.at[3], sib)
    cp_e = local(e_hbm.at[:, pl.ds(mine, half)], e_all.at[pl.ds(0, rows)], ld.at[4])
    hb = blk // 2
    hr = rows // 2

    def product(h):
        f = dot(d[h * hr : (h + 1) * hr], w[...]) + dot_t(lt[:, h * hr : (h + 1) * hr], rt[...])
        snd[h] = f.astype(BF16)
        own[h] = f

    def send_parts(h):
        for i, q in enumerate(VAR):
            to = var_of(*q)
            rs[q, h] = remote(
                snd.at[h, pl.ds(pl.multiple_of(to * hb, hb), hb)], rs_buf.at[i, h], rs_s.at[i, h], rs_r.at[i, h], (samp, to)
            )

    rs = {}
    product(0)
    send_parts(0)
    product(1)
    for cp in st:
        cp.wait_recv()
    t = st_src[var]
    for i in range(len(VAR)):
        t = t + st_buf[i]
    t = jnp.where(low, t, count)
    t_src[...] = t
    zs = [
        remote(t_src, z_buf.at[i], z_s.at[i], z_r.at[i], (samp_of(q, 0, 0), var)) for i, q in enumerate(ZD)
    ]
    send_parts(1)
    cp_e.wait()
    e_own = dot(oh, e_all[pl.ds(0, rows)])
    cp_e2.wait_recv()
    cp_co2.wait_recv()
    oh2 = (co[1] == cohorts).astype(F32).astype(BF16)
    e_sib = dot(oh2, e_all[pl.ds(rows, rows)])

    ag, sb = {}, {}

    def spread_part(h):
        for q in VAR:
            rs[q, h].wait_recv()
        s = own[h, pl.ds(pl.multiple_of(var * hb, hb), hb)]
        for i in range(len(VAR)):
            s = s + rs_buf[i, h].astype(F32)
        row = pl.multiple_of(h * hr + var * hb, hb)
        x_all[pl.ds(row, hb)] = s.astype(BF16)
        for i, q in enumerate(VAR):
            ag[i, h] = remote(
                x_all.at[pl.ds(row, hb)], x_all.at[pl.ds(row, hb)], ag_s.at[i, h], ag_r.at[i, h], (samp, var_of(*q))
            )
        sb[7, h] = share(7, h, row)

    def share(i, h, row):
        return remote(
            x_all.at[pl.ds(row, hb)], x_all.at[pl.ds(pl.multiple_of(rows + row, hb), hb)], sb_s.at[i, h], sb_r.at[i, h], sib
        )

    for cp in zs:
        cp.wait_recv()
    t2 = t
    for i in range(len(ZD)):
        t2 = t2 + z_buf[i]
    t2_src[...] = t2
    ycs = [
        remote(t2_src, yc_buf.at[i], yc_s.at[i], yc_r.at[i], (samp_of(0, *q), var)) for i, q in enumerate(YC)
    ]
    spread_part(0)
    spread_part(1)

    def pass_on(h):
        for i in range(len(VAR) - 1, -1, -1):
            dx, dl = VAR[i]
            ag[i, h].wait_recv()
            sb[i, h] = share(i, h, pl.multiple_of(h * hr + var_of(-dx, -dl) * hb, hb))

    def multiply(h):
        own_half = dot_t(x_all[h * hr : (h + 1) * hr], e_all[h * hr : (h + 1) * hr])
        for i in range(8):
            sb[i, h].wait_recv()
        lo = rows + h * hr
        return own_half + dot_t(x_all[lo : lo + hr], e_all[lo : lo + hr])

    pass_on(0)
    for cp in ycs:
        cp.wait_recv()
    t3 = t2
    for i in range(len(YC)):
        t3 = t3 + yc_buf[i]
    mean = t3 / pltpu.roll(t3, 64, 1)
    d_src[...] = jnp.where(low, t / jnp.maximum(count, 1.0) - mean, 0.0)
    dm[0, var] = d_src[...]
    dms = []
    for i, q in enumerate(VAR):
        for dc in range(NC):
            n = 2 * i + dc
            dms.append(
                remote(d_src, dm.at[dc, var], dm_s.at[n], dm_r.at[n], (samp_of(0, 0, dc), var_of(*q)))
            )
    dms.append(remote(d_src, dm.at[1, var], dm_s.at[14], dm_r.at[14], sib))

    cross[...] = multiply(0)
    pass_on(1)
    cross[...] += multiply(1)
    for cp in dms:
        cp.wait_recv()

    def spread_out(i):
        return jnp.concatenate(
            [jnp.where(low, dm[i, 2 * j], pltpu.roll(dm[i, 2 * j + 1], 64, 1)) for j in range(nv // 2)], axis=1
        )

    d_own = spread_out(0)
    d2 = [split2(d_own), split2(spread_out(1))]
    e2 = [split2(e_own), split2(e_sib)]
    left = jnp.concatenate([d2[i][a] for i in range(2) for a in range(2) for b in range(2)], axis=0)
    right = jnp.concatenate([e2[i][b] for i in range(2) for a in range(2) for b in range(2)], axis=0)
    full = cross[...] + dot_t(left, right)
    cross[...] = full
    cb[...] = full.astype(BF16)
    sub = zrows // NY

    def chunk_rows(dest, dy):
        return pl.ds(pl.multiple_of((dest % NZ) * zrows + ((y + dy) % NY) * sub, sub), sub)

    def hop(i, n, to, src):
        return remote(
            src, zx_buf.at[i, n], zx_s.at[i, n], zx_r.at[i, n], (samp_of(to, 0, 0), var)
        )

    zx = {}

    def far_blocks(i):
        dy = DY[i]
        turn = 1 if i % 2 == 0 else -1
        zx[i, 0] = hop(i, 0, 2 * turn, cb.at[chunk_rows(z + 4, dy)])
        zx[i, 1] = hop(i, 1, 1, cb.at[chunk_rows(z + 3, dy)])
        zx[i, 2] = hop(i, 2, -1, cb.at[chunk_rows(z + NZ - 3, dy)])

    def near_blocks(i):
        dy = DY[i]
        zx[i, 5] = hop(i, 5, 1, cb.at[chunk_rows(z + 1, dy)])
        zx[i, 6] = hop(i, 6, -1, cb.at[chunk_rows(z + NZ - 1, dy)])

    for i in range(3):
        far_blocks(i)
    for i in range(3):
        near_blocks(i)
    far_blocks(3)

    xo = x_all[pl.ds(0, rows)]
    xf = xo.astype(F32)
    resid = dot(oh, xo)
    q = jnp.sum(xf * xf, axis=0, keepdims=True)
    q = q + jnp.sum(d_own * (2.0 * resid + count * d_own), axis=0, keepdims=True)
    q_src[...] = jnp.concatenate([q[:, j * 128 : (j + 1) * 128] for j in range(k // 128)] * 2, axis=0)
    qy = [
        remote(q_src, q_yc.at[i], qy_s.at[i], qy_r.at[i], (samp_of(0, *a), var)) for i, a in enumerate(YC)
    ]
    for i, dy in enumerate(DY):
        turn = 1 if i % 2 == 0 else -1
        for n in range(3):
            zx[i, n].wait_recv()
        for a, way in enumerate((1, -1)):
            part = cross[chunk_rows(z + 2 * way + NZ, dy)] + zx_buf[i, 1 + a].astype(F32)
            if way == turn:
                part = part + zx_buf[i, 0].astype(F32)
            zx_src[i, a] = part.astype(BF16)
            zx[i, 3 + a] = hop(i, 3 + a, 2 * way, zx_src.at[i, a])
    near_blocks(3)
    for cp in qy:
        cp.wait_recv()
    q2 = q_src[...]
    for i in range(len(YC)):
        q2 = q2 + q_yc[i]
    q2_src[...] = q2
    qz = [
        remote(q2_src, q_z.at[i], qz_s.at[i], qz_r.at[i], (samp_of(b, 0, 0), var)) for i, b in enumerate(ZD)
    ]
    yx = {}
    for i, dy in enumerate(DY):
        acc = cross[chunk_rows(z, dy)]
        for n in (5, 6, 3, 4):
            zx[i, n].wait_recv()
            acc = acc + zx_buf[i, n].astype(F32)
        if dy == 0:
            own_y[0] = acc[:8]
            own_y[1] = acc[8:]
        ysrc[i, 0] = acc[:8].astype(BF16)
        ysrc[i, 1] = acc[8:].astype(BF16)
        for dc in (1, 0):
            if dy or dc:
                m = YC.index((dy, dc))
                yx[m] = remote(
                    ysrc.at[i, (c + dc) % NC], yx_buf.at[m], yx_s.at[m], yx_r.at[m], (samp_of(0, dy, dc), var)
                )
    yx = [yx[m] for m in range(len(YC))]
    zx, rs, ag, sb = [list(group.values()) for group in (zx, rs, ag, sb)]
    for cp in qz:
        cp.wait_recv()
    q3 = q2
    for i in range(len(ZD)):
        q3 = q3 + q_z[i]
    spread = lax.rsqrt(q3[:4] / total + 1e-6) / total
    spread = jnp.concatenate([spread[j : j + 1] for j in range(4)], axis=1)
    at_row = lax.broadcasted_iota(jnp.int32, (8, k), 1) - samp * 8 == lax.broadcasted_iota(jnp.int32, (8, k), 0)
    scale = jnp.sum(jnp.where(at_row, spread, 0.0), axis=1, keepdims=True)

    for cp in yx:
        cp.wait_recv()
    same = own_y[c]
    cross_half = jnp.zeros_like(same)
    for i, (dy, dc) in enumerate(YC):
        if dc:
            cross_half = cross_half + yx_buf[i].astype(F32)
        else:
            same = same + yx_buf[i].astype(F32)
    o_ref[:, pl.ds(mine, half)] = same * scale
    o_ref[:, pl.ds(other, half)] = cross_half * scale

    for cp in [cp_e2, cp_co2] + st + rs + ycs + ag + sb + zs + dms + zx + qy + qz + yx:
        cp.wait_send()


def shards(total, dosages, weights, prior, cohort, expression):
    rows, depth = dosages.shape
    k = weights.shape[1]
    genes = expression.shape[1]
    half = genes // 2
    width = prior.shape[1]
    blk = rows // 8
    out_rows = k // 64
    vm, sem = pltpu.VMEM, pltpu.SemaphoreType.DMA
    scratch = [
        vm((rows, depth), BF16), vm((depth, k), BF16), vm((width, rows), F32), vm((2, 1, rows), jnp.int32),
        vm((2 * rows, half), BF16), vm((3 * width + 4 * COHORTS, rows), BF16), vm((3 * width + 4 * COHORTS, k), BF16),
        vm((2, rows // 2, k), BF16), vm((2, rows // 2, k), F32), vm((7, 2, blk // 2, k), BF16), vm((2 * rows, k), BF16),
        vm((8, COHORTS, 128), F32), vm((7, COHORTS, 128), F32), vm((COHORTS, 128), F32), vm((7, COHORTS, 128), F32),
        vm((COHORTS, 128), F32), vm((7, COHORTS, 128), F32),
        vm((COHORTS, 128), F32), vm((2, 8, COHORTS, 128), F32), vm((k, half), F32), vm((k, half), BF16),
        vm((4, 7, k // 32, half), BF16), vm((4, 2, k // 32, half), BF16), vm((2, out_rows, half), F32), vm((4, 2, out_rows, half), BF16), vm((7, out_rows, half), BF16),
        vm((8, 128), F32), vm((7, 8, 128), F32), vm((8, 128), F32), vm((7, 8, 128), F32),
        sem((5,)), sem((4,)), sem((7,)), sem((7,)), sem((7,)), sem((7,)), sem((7,)), sem((7,)),
        sem((15,)), sem((15,)), sem((7, 2)), sem((7, 2)), sem((7, 2)), sem((7, 2)), sem((8, 2)), sem((8, 2)),
        sem((4, 7)), sem((4, 7)), sem((7,)), sem((7,)), sem((7,)), sem((7,)), sem((7,)), sem((7,)),
    ]
    return pl.pallas_call(
        functools.partial(kernel, float(total)),
        out_shape=jax.ShapeDtypeStruct((out_rows, genes), F32),
        in_specs=[pl.BlockSpec(memory_space=pl.ANY)] * 5,
        out_specs=pl.BlockSpec(memory_space=pltpu.VMEM),
        scratch_shapes=scratch,
        compiler_params=pltpu.CompilerParams(
            collective_id=0, has_side_effects=True, vmem_limit_bytes=67043328
        ),
    )(dosages, weights, prior.T, cohort.reshape(1, rows), expression)


def solution(mesh):
    placed = (P("samp", "var"), P("var", None), P("samp", "var"), P("samp", None), P("samp", "var"))

    def run(dosages, weights, prior, cohort, expression):
        body = functools.partial(shards, dosages.shape[0])
        return jax.shard_map(body, mesh=mesh, in_specs=placed, out_specs=P("samp", "var"), check_vma=False)(
            dosages, weights, prior, cohort, expression
        )

    return run
```
